32 devices in a mesh: shard: 8 (over z, core), replica: 4 (over y, x).
Axes of the slice: x: 2, y: 2, z: 4, core: 2. Of those that a mesh axis runs over, the one named last changes fastest.
Arguments:
- block_in: bfloat16 [4, 1024, 2048], P('replica', 'shard'), may hold values from -6 to 6
- norm_gain: bfloat16 [2048], P('shard'), may hold values from 0.099609375 to 1.8984375
- norm_bias: bfloat16 [2048], P('shard'), may hold values from -3 to 3
- attn_weight: bfloat16 [2048, 6144], P('shard'), may hold values from -0.125 to 0.125
- attn_bias: bfloat16 [6144], P('shard'), may hold values from -3 to 3
- dense_weight: bfloat16 [2048, 2048], P('shard'), may hold values from -0.5 to 0.5
- dense_bias: bfloat16 [2048], P('shard'), may hold values from -3 to 3
- up_weight: bfloat16 [2048, 8192], P('shard'), may hold values from -0.125 to 0.125
- up_bias: bfloat16 [8192], P('shard'), may hold values from -3 to 3
- down_weight: bfloat16 [8192, 2048], P('shard'), may hold values from -0.0625 to 0.0625
- down_bias: bfloat16 [2048], P('shard'), may hold values from -3 to 3
- cotangent: bfloat16 [4, 1024, 2048], P('replica', 'shard'), may hold values from -6 to 6
Outputs:
- block_out: bfloat16 [4, 1024, 2048], P('replica', 'shard')
- grad_in: bfloat16 [4, 1024, 2048], P('replica', 'shard')
- grad_norm_gain: float32 [2048], P('shard')
- grad_norm_bias: float32 [2048], P('shard')
- grad_attn_weight: float32 [2048, 6144], P('shard')
- grad_attn_bias: float32 [6144], P('shard')
- grad_dense_weight: float32 [2048, 2048], P('shard')
- grad_dense_bias: float32 [2048], P('shard')
- grad_up_weight: float32 [2048, 8192], P('shard')
- grad_up_bias: float32 [8192], P('shard')
- grad_down_weight: float32 [8192, 2048], P('shard')
- grad_down_bias: float32 [2048], P('shard')
The draws below stay inside these ranges and needn't reach their ends.
All inputs are finite; a program needn't handle non-finite values.
Results may differ from the reference program's by a relative error of at most 0.018.
Values may be sent and summed in bfloat16 or wider, within the bound.
No kernel may reach another device: no remote copies, remote signals or barrier semaphores. Data moves between devices by JAX's collectives and lax.ppermute only.
A program may use at most 704 MiB of HBM per device.

```python
import math
import jax
import jax.numpy as jnp
from jax import lax

D = 2048
H = 32
HD = 64
ROT = 32
FF = 8192
SEQS = 4
LENGTH = 1024


def block_levels(own_key, shape, cuts, least, high):
    level = 1.0
    for dim, parts in cuts:
        draws = jax.random.uniform(jax.random.fold_in(jax.random.fold_in(own_key, 6), dim), (parts,), jnp.float32, least / len(cuts), high / len(cuts))
        level = level * jnp.repeat(jnp.exp(draws), shape[dim] // parts).reshape((-1,) + (1,) * (len(shape) - 1 - dim))
    return level


def bell_draw(stream_key, dims, deviation, bound, pieces=(), kind=jnp.bfloat16):
    loudness = block_levels(stream_key, dims, pieces, -0.22, 0.18) if pieces else 1.0
    values = jax.random.normal(stream_key, dims, jnp.float32) * deviation * loudness
    return jnp.minimum(jnp.maximum(values, -bound), bound).astype(kind)


def setup_inputs(seed: int = 0) -> dict:
    arg_keys = jax.random.split(jax.random.key(seed), 13)
    return {
        "block_in": bell_draw(arg_keys[0], (SEQS, LENGTH, D), 1.0, 6.0, ((0, 4), (1, 8))),
        "norm_gain": jnp.clip(1.0 + 0.18 * jax.random.normal(arg_keys[1], (D,), jnp.float32), 0.099609375, 1.8984375).astype(jnp.bfloat16),
        "norm_bias": bell_draw(arg_keys[2], (D,), 0.5, 3.0, ((0, 8),)),
        "attn_weight": bell_draw(arg_keys[3], (D, 3 * D), D ** -0.5, 0.125, ((0, 8),)),
        "attn_bias": bell_draw(arg_keys[4], (3 * D,), 0.5, 3.0, ((0, 8),)),
        "dense_weight": bell_draw(arg_keys[5], (D, D), (D // 16) ** -0.5, 0.5, ((0, 8),)),
        "dense_bias": bell_draw(arg_keys[6], (D,), 0.5, 3.0, ((0, 8),)),
        "up_weight": bell_draw(arg_keys[7], (D, FF), D ** -0.5, 0.125, ((0, 8),)),
        "up_bias": bell_draw(arg_keys[8], (FF,), 0.5, 3.0, ((0, 8),)),
        "down_weight": bell_draw(arg_keys[9], (FF, D), FF ** -0.5, 0.0625, ((0, 8),)),
        "down_bias": bell_draw(arg_keys[10], (D,), 0.5, 3.0, ((0, 8),)),
        "cotangent": bell_draw(arg_keys[11], (SEQS, LENGTH, D), 1.0, 6.0, ((0, 4), (1, 8))),
    }


EPSILON = 1e-05
ROPE_BASE = 10000.0
MASK_VALUE = -1e+30

@jax.custom_vjp
def low(v):
    return lax.optimization_barrier(v.astype(jnp.bfloat16)).astype(jnp.float32)

@jax.custom_vjp
def low_back(v):
    return v

def low_keep(v):
    return (low(v), None)

def low_pass(kept, grad):
    return (grad,)

def back_keep(v):
    return (v, None)

def back_low(kept, grad):
    return (low(grad),)
low.defvjp(low_keep, low_pass)
low_back.defvjp(back_keep, back_low)

def layer_norm(values, norm_gain, norm_shift):
    center = values - lax.optimization_barrier(jnp.mean(values, axis=-1, keepdims=True))
    spread = lax.optimization_barrier(jnp.mean(center * center, axis=-1, keepdims=True))
    return center * lax.rsqrt(spread + EPSILON) * norm_gain + norm_shift

def rotate(values, positions):
    half_rot = ROT // 2
    frequencies = ROPE_BASE ** (-2.0 * jnp.arange(half_rot, dtype=jnp.float32) / ROT)
    angles = positions[:, None] * frequencies[None, :]
    cosine_rows = jnp.cos(angles)[:, None, :]
    sine_rows = jnp.sin(angles)[:, None, :]
    first_half = values[..., :half_rot]
    second_half = values[..., half_rot:ROT]
    return jnp.concatenate([first_half * cosine_rows - second_half * sine_rows, second_half * cosine_rows + first_half * sine_rows, values[..., ROT:]], axis=-1)

def attend_sequence(triple):
    queries, keys, values = triple
    seq_len = queries.shape[0]
    block_rows = math.gcd(seq_len, 512)
    key_pos = jnp.arange(seq_len, dtype=jnp.int32)
    score_scale = HD ** (-0.5)

    def one_block(block_index):
        query_rows = lax.dynamic_slice_in_dim(queries, block_index * block_rows, block_rows, 0)
        scores = jnp.einsum('qhd,khd->hqk', query_rows, keys, precision=lax.Precision.HIGHEST) * score_scale
        scores = low_back(scores)
        query_pos = block_index * block_rows + jnp.arange(block_rows, dtype=jnp.int32)
        allowed = key_pos[None, :] <= query_pos[:, None]
        scores = jnp.where(allowed[None], scores, MASK_VALUE)
        weights = low(jax.nn.softmax(scores, axis=-1))
        return jnp.einsum('hqk,khd->qhd', weights, values, precision=lax.Precision.HIGHEST)
    outputs = lax.map(jax.checkpoint(one_block), jnp.arange(seq_len // block_rows, dtype=jnp.int32))
    return outputs.reshape(seq_len, H, HD)

def forward(block_in, norm_gain, norm_bias, attn_weight, attn_bias, dense_weight, dense_bias, up_weight, up_bias, down_weight, down_bias):
    seq_count, seq_len = (block_in.shape[0], block_in.shape[1])
    normed = low(layer_norm(block_in, norm_gain, norm_bias))
    projected = low_back(jnp.dot(normed, attn_weight, precision=lax.Precision.HIGHEST) + attn_bias)
    queries = projected[..., :D].reshape(seq_count, seq_len, H, HD)
    keys = projected[..., D:2 * D].reshape(seq_count, seq_len, H, HD)
    values = projected[..., 2 * D:].reshape(seq_count, seq_len, H, HD)
    positions = jnp.arange(seq_len, dtype=jnp.float32)
    rot_queries = low(rotate(queries, positions))
    rot_keys = low(rotate(keys, positions))
    mixed_rows = lax.map(jax.checkpoint(attend_sequence), (rot_queries, rot_keys, low(values)))
    mixed_rows = low(low_back(mixed_rows.reshape(seq_count, seq_len, D)))
    attn_branch = jnp.dot(mixed_rows, dense_weight, precision=lax.Precision.HIGHEST) + dense_bias
    hidden_pre = low_back(jnp.dot(normed, up_weight, precision=lax.Precision.HIGHEST) + up_bias)
    hidden = low(jax.nn.gelu(hidden_pre, approximate=True))
    mlp_branch = jnp.dot(hidden, down_weight, precision=lax.Precision.HIGHEST) + down_bias
    return block_in + attn_branch + mlp_branch

def reference(block_in, norm_gain, norm_bias, attn_weight, attn_bias, dense_weight, dense_bias, up_weight, up_bias, down_weight, down_bias, cotangent):
    inputs = [array.astype(jnp.float32) for array in (block_in, norm_gain, norm_bias, attn_weight, attn_bias, dense_weight, dense_bias, up_weight, up_bias, down_weight, down_bias)]
    result, pull_back = jax.vjp(forward, *inputs)
    gradients = pull_back(cotangent.astype(jnp.float32))
    return (result.astype(jnp.bfloat16), gradients[0].astype(jnp.bfloat16), gradients[1], gradients[2], gradients[3], gradients[4], gradients[5], gradients[6], gradients[7], gradients[8], gradients[9], gradients[10])
```

```python
import functools

import jax
import jax.numpy as jnp
from jax import lax
from jax.experimental import pallas as pl
from jax.experimental.pallas import tpu as pltpu
from jax.sharding import PartitionSpec as P

D = 2048
H = 32
HD = 64
ROT = 32
FF = 8192

EPSILON = 1e-05
ROPE_BASE = 10000.0
MASK_VALUE = -1e30
F32 = jnp.float32
BF16 = jnp.bfloat16
GELU_C = 0.7978845608028654


def dot(left, right, contract=(1, 0)):
    return lax.dot_general(
        left, right, (((contract[0],), (contract[1],)), ((), ())), preferred_element_type=F32
    )


def chip_shift(shard_count, k):
    chips = shard_count // 2
    return [(2 * z + c, 2 * ((z + k) % chips) + c) for z in range(chips) for c in range(2)]


def flip(count, mask):
    return [(i, i ^ mask) for i in range(count)]


def gather_tokens(rows):
    count = lax.axis_size("shard")
    pieces = [rows]
    for k in range(1, count // 2):
        pieces.append(lax.ppermute(rows, "shard", chip_shift(count, k)))
    near = jnp.concatenate(pieces, axis=0)
    far = lax.ppermute(near, "shard", flip(count, 1))
    return jnp.concatenate([near, far], axis=0)


def scatter_tokens(partial):
    count = lax.axis_size("shard")
    chips = count // 2
    half = partial.shape[0] // 2
    rows = half // chips
    got = lax.ppermute(partial[half:].astype(BF16), "shard", flip(count, 1))
    near = partial[:half] + got.astype(F32)
    total = near[:rows]
    for k in range(1, chips):
        piece = near[k * rows : (k + 1) * rows].astype(BF16)
        total = total + lax.ppermute(piece, "shard", chip_shift(count, -k)).astype(F32)
    return total


def replica_bits():
    return list(range(lax.axis_size("replica").bit_length() - 1))


def scatter_replicas(pieces, bits):
    count = lax.axis_size("replica")
    held = dict(enumerate(pieces))
    for b in bits:
        m = 1 << b
        keep = [p for p in held if not p & m]
        got = [lax.ppermute(held[p | m], "replica", flip(count, m)) for p in keep]
        held = {p: (held[p].astype(F32) + g.astype(F32)).astype(BF16) for p, g in zip(keep, got)}
    return held[0]


def gather_replicas(piece, bits):
    count = lax.axis_size("replica")
    held = {0: piece}
    for b in bits:
        m = 1 << b
        got = {p | m: lax.ppermute(a, "replica", flip(count, m)) for p, a in held.items()}
        held.update(got)
    return [held[p] for p in range(count)]


def swap_order(pieces):
    index = lax.axis_index("replica")
    stacked = jnp.stack(pieces) if isinstance(pieces, list) else pieces
    return [
        lax.dynamic_index_in_dim(stacked, index ^ p, 0, keepdims=False)
        for p in range(stacked.shape[0])
    ]


def exchange(blocks):
    return lax.all_to_all(blocks, "shard", 0, 0, tiled=True)


def attention_kernel(
    order_ref, q_ref, k_ref, v_ref, g_ref, cos_ref, lo_ref, hi_ref,
    mix_ref, gq_ref, gk_ref, gv_ref,
    q_sc, k_sc, v_sc, g_sc, dk_sc, dv_sc,
    *, blocks, block, step,
):
    tokens = blocks * block
    scale = HD**-0.5
    lanes = 2 * HD

    def turn(x, at, sign):
        cos, lo, hi = cos_ref[at, :], lo_ref[at, :], hi_ref[at, :]
        up = pltpu.roll(x, lanes - ROT // 2, 1)
        down = pltpu.roll(x, ROT // 2, 1)
        return x * cos + sign * (up * lo + down * hi)

    for b in range(blocks):
        src = pl.ds(pl.multiple_of(order_ref[b] * block, block), block)
        dst = pl.ds(b * block, block)
        q_sc[dst, :] = turn(q_ref[src, :], dst, 1.0).astype(BF16)
        k_sc[dst, :] = turn(k_ref[src, :], dst, 1.0).astype(BF16)
        v_sc[dst, :] = v_ref[src, :].astype(BF16)
        g_sc[dst, :] = g_ref[src, :]
    dk_sc[...] = jnp.zeros_like(dk_sc)
    dv_sc[...] = jnp.zeros_like(dv_sc)
    lane = lax.broadcasted_iota(jnp.int32, (1, lanes), 1)
    heads = [lane < HD, lane >= HD]
    for i in range(tokens // step):
        rows = pl.ds(i * step, step)
        width = (i + 1) * step
        q, g = q_sc[rows, :], g_sc[rows, :]
        k, v = k_sc[:width, :], v_sc[:width, :]
        seen = lax.broadcasted_iota(jnp.int32, (step, width), 1) <= i * step + (
            lax.broadcasted_iota(jnp.int32, (step, width), 0)
        )
        mixed = jnp.zeros((step, lanes), F32)
        dq = jnp.zeros((step, lanes), F32)
        for mine in heads:
            zero = jnp.zeros((), BF16)
            qh, gh = jnp.where(mine, q, zero), jnp.where(mine, g, zero)
            scores = dot(qh, k, (1, 1)) * scale
            scores = jnp.where(seen, scores, MASK_VALUE)
            top = jnp.max(scores, axis=1, keepdims=True)
            raised = jnp.exp(scores - top)
            probs = raised / jnp.sum(raised, axis=1, keepdims=True)
            weights = probs.astype(BF16)
            mixed = jnp.where(mine, dot(weights, v), mixed)
            grad_probs = dot(gh, v, (1, 1))
            delta = jnp.sum(probs * grad_probs, axis=1, keepdims=True)
            grad_scores = (probs * (grad_probs - delta)).astype(BF16)
            dq = jnp.where(mine, dot(grad_scores, k), dq)
            dk_sc[:width, :] += dot(grad_scores, qh, (0, 0))
            dv_sc[:width, :] += dot(weights, gh, (0, 0))
        dq = turn(dq * scale, rows, -1.0).astype(BF16)
        mixed = mixed.astype(BF16)
        for j in range(step // block):
            b = i * (step // block) + j
            out = pl.ds(pl.multiple_of(order_ref[b] * block, block), block)
            mix_ref[out, :] = mixed[j * block : (j + 1) * block]
            gq_ref[out, :] = dq[j * block : (j + 1) * block]
    for b in range(blocks):
        src = pl.ds(b * block, block)
        out = pl.ds(pl.multiple_of(order_ref[b] * block, block), block)
        gk_ref[out, :] = turn(dk_sc[src, :] * scale, src, -1.0).astype(BF16)
        gv_ref[out, :] = dv_sc[src, :].astype(BF16)


def attention(projected, grad_mixed, order, block):
    tokens, width = grad_mixed.shape
    lanes = 2 * HD
    pairs = width // lanes
    positions = jnp.arange(tokens, dtype=F32)
    frequencies = ROPE_BASE ** (-2.0 * jnp.arange(ROT // 2, dtype=F32) / ROT)
    angles = positions[:, None] * frequencies[None, :]
    cosine, sine = jnp.cos(angles), jnp.sin(angles)
    none, rest = jnp.zeros_like(sine), jnp.zeros((tokens, HD - ROT), F32)
    cos = jnp.concatenate([cosine, cosine, rest + 1.0] * 2, axis=1)
    low = jnp.concatenate([-sine, none, rest] * 2, axis=1)
    high = jnp.concatenate([none, sine, rest] * 2, axis=1)
    step = min(256, tokens)

    def column(offset):
        return pl.BlockSpec((tokens, lanes), lambda h, o: (0, offset + h))

    whole = pl.BlockSpec((tokens, lanes), lambda h, o: (0, 0))
    shape = jax.ShapeDtypeStruct((tokens, width), BF16)
    return pl.pallas_call(
        functools.partial(attention_kernel, blocks=tokens // block, block=block, step=step),
        out_shape=(shape,) * 4,
        grid_spec=pltpu.PrefetchScalarGridSpec(
            num_scalar_prefetch=1,
            grid=(pairs,),
            in_specs=[column(0), column(pairs), column(2 * pairs), column(0), whole, whole, whole],
            out_specs=[column(0)] * 4,
            scratch_shapes=[pltpu.VMEM((tokens, lanes), BF16)] * 4
            + [pltpu.VMEM((tokens, lanes), F32)] * 2,
        ),
        compiler_params=pltpu.CompilerParams(vmem_limit_bytes=48 * 2**20),
        cost_estimate=pl.CostEstimate(
            flops=14 * tokens * tokens * width,
            bytes_accessed=24 * tokens * width,
            transcendentals=tokens * tokens * (width // HD) // 2,
        ),
        name="attention",
    )(order, projected, projected, projected, grad_mixed, cos, low, high)


def normalize(values):
    center = values - jnp.mean(values, axis=-1, keepdims=True)
    spread = jnp.mean(center * center, axis=-1, keepdims=True)
    inverse = lax.rsqrt(spread + EPSILON)
    return center * inverse, inverse


def gelu_and_slope(u):
    inner = GELU_C * (u + 0.044715 * u * u * u)
    t = jnp.tanh(inner)
    slope = 0.5 * (1.0 + t) + 0.5 * u * (1.0 - t * t) * GELU_C * (1.0 + 3 * 0.044715 * u * u)
    return 0.5 * u * (1.0 + t), slope


def shards(
    block_in,
    norm_gain,
    norm_bias,
    attn_weight,
    attn_bias,
    dense_weight,
    dense_bias,
    up_weight,
    up_bias,
    down_weight,
    down_bias,
    cotangent,
):
    own, upstream = block_in[0], cotangent[0]
    tok_rows = own.shape[0]
    count, copies = lax.axis_size("shard"), lax.axis_size("replica")
    shard, replica = lax.axis_index("shard"), lax.axis_index("replica")
    chips = count // 2
    width = attn_weight.shape[0]
    ff = down_weight.shape[0]
    ff_part, row_part = ff // copies, width // copies
    bits = replica_bits()
    back = bits[::-1]

    up_part = lax.dynamic_index_in_dim(
        up_weight.reshape(width, count, copies, ff_part), replica, 2, keepdims=False
    )
    up_part = exchange(up_part.transpose(1, 0, 2)).reshape(D, ff_part)
    up_pieces = gather_replicas(up_part, bits)
    up_mine = jnp.concatenate(up_pieces, axis=1)
    attn_part = lax.dynamic_slice_in_dim(attn_weight, replica * row_part, row_part, 0)
    attn_part = attn_part.reshape(row_part, 3, count, width).transpose(2, 0, 1, 3)
    attn_part = exchange(attn_part.reshape(count, row_part, 3 * width))
    attn_mine = jnp.stack(swap_order(gather_replicas(attn_part, back)), axis=1)
    attn_mine = attn_mine.reshape(D, 3 * width)
    down_mine = jnp.concatenate(swap_order(down_weight.reshape(copies, ff_part, D)), axis=0)
    up_bias_mine = jnp.concatenate(swap_order(up_bias.reshape(copies, ff_part)))

    packed = jnp.concatenate(
        [
            norm_gain[:, None],
            norm_bias[:, None],
            attn_bias.reshape(width, 3),
            dense_bias[:, None],
            down_bias[:, None],
        ],
        axis=1,
    )
    small = lax.all_gather(packed, "shard", axis=0, tiled=True).astype(F32)
    gain, shift = small[:, 0], small[:, 1]
    attn_bias_full = small[:, 2:5].reshape(3, count, width)
    attn_bias_mine = lax.dynamic_index_in_dim(attn_bias_full, shard, 1, keepdims=False)
    out_bias = small[:, 5] + small[:, 6]

    tokens = gather_tokens(own).astype(F32)
    grads = gather_tokens(upstream)
    normed = (normalize(tokens)[0] * gain + shift).astype(BF16)

    hidden_pre = dot(normed, up_mine) + up_bias_mine.astype(F32)
    hidden, slope = gelu_and_slope(hidden_pre)
    hidden = hidden.astype(BF16)
    grad_pre = (dot(grads, down_mine, (1, 1)) * slope).astype(BF16)
    grad_down = [
        dot(hidden[:, p * ff_part : (p + 1) * ff_part], grads, (0, 0)).astype(BF16)
        for p in range(copies)
    ]
    grad_up = [
        dot(normed, grad_pre[:, p * ff_part : (p + 1) * ff_part], (0, 0)).astype(BF16)
        for p in range(copies)
    ]
    grad_down = gather_replicas(scatter_replicas(grad_down, bits), back)
    grad_up = scatter_replicas(grad_up, back)
    grad_up = exchange(grad_up.reshape(count, width, ff_part))
    grad_up = gather_replicas(grad_up, bits)

    projected = dot(normed, attn_mine) + attn_bias_mine.reshape(-1)
    grad_mixed = dot(grads, dense_weight, (1, 1)).astype(BF16)
    z, c = shard // 2, shard % 2
    place = jnp.arange(count, dtype=jnp.int32)
    order = ((place % 2) ^ c) * chips + (z - place // 2) % chips
    mixed, grad_q, grad_k, grad_v = attention(projected, grad_mixed, order, tok_rows)
    grad_projected = jnp.concatenate([grad_q, grad_k, grad_v], axis=1)
    grad_dense = dot(mixed, grads, (0, 0)).astype(BF16).reshape(copies, row_part, D)
    grad_dense = gather_replicas(scatter_replicas(swap_order(grad_dense), bits), back)
    grad_attn = dot(normed, grad_projected, (0, 0)).astype(BF16)
    grad_attn = grad_attn.reshape(count, copies, row_part, 3 * width).transpose(1, 0, 2, 3)
    grad_attn = swap_order(grad_attn)
    half = 3 * width // 2
    attn_halves = []
    for h, (first, second) in enumerate(((bits, back), (back, bits))):
        piece = scatter_replicas([a[..., h * half : (h + 1) * half] for a in grad_attn], first)
        attn_halves.append(gather_replicas(exchange(piece), second))

    branches = scatter_tokens(dot(hidden, down_mine) + dot(mixed, dense_weight))
    inputs = own.astype(F32)
    block_out = (inputs + branches + out_bias).astype(BF16)[None]
    part_rows = scatter_tokens(dot(grad_projected, attn_mine, (1, 1)) + dot(grad_pre, up_mine, (1, 1)))
    xhat, inverse = normalize(inputs)
    scaled = part_rows * gain
    grad_inputs = inverse * (
        scaled
        - jnp.mean(scaled, axis=-1, keepdims=True)
        - xhat * jnp.mean(scaled * xhat, axis=-1, keepdims=True)
    )
    grad_in = (upstream.astype(F32) + grad_inputs).astype(BF16)[None]

    sum_attn = jnp.sum(grad_projected.astype(F32), axis=0).reshape(3, 1, width)
    sum_up = jnp.sum(grad_pre.astype(F32), axis=0).reshape(copies, ff_part)
    sum_up = jnp.concatenate(swap_order(sum_up))
    sums = jnp.concatenate(
        [
            jnp.sum(part_rows * xhat, axis=0),
            jnp.sum(part_rows, axis=0),
            jnp.sum(upstream.astype(F32), axis=0),
            lax.dynamic_update_slice(jnp.zeros((3, count, width), F32), sum_attn, (0, shard, 0)).reshape(-1),
            lax.dynamic_update_slice(jnp.zeros((FF,), F32), sum_up, (shard * ff,)),
        ]
    )
    sums = lax.psum(sums, ("shard", "replica"))

    def mine(start, size):
        return lax.dynamic_slice(sums, (start + shard * size,), (size,))

    grad_out_bias = mine(2 * D, width)

    attn_whole = [jnp.stack(swap_order(a)) for a in attn_halves]
    attn_whole = jnp.concatenate(attn_whole, axis=-1)
    attn_whole = attn_whole.reshape(copies, count, row_part, 3, width).transpose(0, 2, 3, 1, 4)
    up_whole = jnp.stack(swap_order(grad_up)).transpose(2, 1, 0, 3)
    return (
        block_out,
        grad_in,
        mine(0, width),
        mine(D, width),
        attn_whole.reshape(width, 3 * D).astype(F32),
        mine(3 * D, 3 * width),
        jnp.concatenate(swap_order(grad_dense), axis=0).astype(F32),
        grad_out_bias,
        up_whole.reshape(width, FF).astype(F32),
        mine(6 * D, ff),
        jnp.concatenate(swap_order(grad_down), axis=0).astype(F32),
        grad_out_bias,
    )


def solution(mesh):
    vector, matrix = P("shard"), P("shard", None)
    rows = P("replica", "shard", None)
    return jax.shard_map(
        shards,
        mesh=mesh,
        in_specs=(rows, vector, vector, matrix, vector, matrix, vector, matrix, vector, matrix, vector, rows),
        out_specs=(rows, rows, vector, vector, matrix, vector, matrix, vector, matrix, vector, matrix, vector),
        check_vma=False,
    )
```

```python
import functools

import jax
import jax.numpy as jnp
import numpy as np
from jax import lax
from jax.experimental import pallas as pl
from jax.experimental.pallas import tpu as pltpu
from jax.sharding import PartitionSpec as P

D = 2048
H = 32
HD = 64
ROT = 32
FF = 8192

EPSILON = 1e-05
ROPE_BASE = 10000.0
MASK_VALUE = -1e30
F32 = jnp.float32
BF16 = jnp.bfloat16
GELU_C = 0.7978845608028654
HUGE = 2**38
MEDIUM = 2**27


def dot(left, right, contract=(1, 0)):
    return lax.dot_general(
        left, right, (((contract[0],), (contract[1],)), ((), ())), preferred_element_type=F32
    )


def flip(count, mask):
    return [(i, i ^ mask) for i in range(count)]


def replica_order(bits):
    count = lax.axis_size("replica")
    return sorted(range(count), key=lambda p: [p >> b & 1 for b in bits])


def cross(pair, bit, *hold):
    keep, send = pair
    got = lax.ppermute(send, "replica", flip(lax.axis_size("replica"), 1 << bit))
    return keep, after(got, *hold)


def last_pairs(pairs, orders, *hold):
    out = []
    for pair, bits in zip(pairs, orders):
        for bit in bits[1:-1]:
            pair = add([cross(pair, bit, *hold)])
        out.append(cross(pair, bits[-1], *hold))
    return out


def gather_replicas(piece, bits, *hold):
    count = lax.axis_size("replica")
    held = [piece]
    for b in bits[::-1]:
        got = [lax.ppermute(a, "replica", flip(count, 1 << b)) for a in held]
        held = held + [after(a, *hold) for a in got]
    return held


def spread_replicas(piece):
    count = lax.axis_size("replica")
    return [piece] + [lax.ppermute(piece, "replica", flip(count, p)) for p in range(1, count)]


def exchange(blocks):
    return lax.all_to_all(blocks, "shard", 0, 0, tiled=True)


def after(value, *others):
    return lax.optimization_barrier((value,) + others)[0]


def kernel_call(kernel, *, out_shape, cost=1, **options):
    def in_hbm(array):
        big = array.size * array.dtype.itemsize >= 2**18
        return pltpu.with_memory_space_constraint(array, pltpu.HBM) if big else array

    several = isinstance(out_shape, tuple)
    shapes = [
        pltpu.HBM(a.shape, a.dtype) if a.size * a.dtype.itemsize >= 2**18 else a
        for a in (out_shape if several else (out_shape,))
    ]
    call = pl.pallas_call(
        kernel,
        out_shape=tuple(shapes) if several else shapes[0],
        cost_estimate=pl.CostEstimate(flops=cost, bytes_accessed=cost, transcendentals=0),
        **options,
    )
    return lambda *args: call(*map(in_hbm, args))


def scalar(value):
    return jnp.reshape(value, (1,)).astype(jnp.int32)


def add(pairs, cost=1):
    n, columns = pairs[0][0].shape[0], pairs[0][0].shape[2]
    heights = [left.shape[1] for left, _ in pairs]
    half, rows = max(n // 2, 1), sum(heights)
    block = columns // 2 if columns % 256 == 0 else columns

    def kernel(*refs):
        ins, outs = refs[: 2 * len(pairs)], refs[2 * len(pairs) :]
        at = 0
        for j, height in enumerate(heights):
            for i in range(n):
                total = ins[2 * j][i].astype(F32) + ins[2 * j + 1][i].astype(F32)
                outs[i // half][i % half, at : at + height, :] = total.astype(BF16)
            at += height

    out = jax.ShapeDtypeStruct((half, rows, columns), BF16)
    return kernel_call(
        kernel,
        out_shape=(out,) * (n // half),
        grid=(columns // block,),
        in_specs=[
            pl.BlockSpec((n, height, block), lambda i: (0, 0, i)) for height in heights for _ in "12"
        ],
        out_specs=[pl.BlockSpec((half, rows, block), lambda i: (0, 0, i))] * (n // half),
        compiler_params=pltpu.CompilerParams(vmem_limit_bytes=40 * 2**20),
        cost=cost,
        name="add",
    )(*[x for pair in pairs for x in pair])


def select_rows(weight, replica, count, copies, groups):
    rows, width = weight.shape[0] // copies, weight.shape[1] // (groups * count)
    lanes = width if groups == 1 else 2 * HD

    def kernel(at, weight_ref, out):
        for i in range(count):
            for h in range(width // lanes):
                for g in range(groups):
                    here, to = (g * count + i) * width + h * lanes, (h * groups + g) * lanes
                    out[i, :, to : to + lanes] = weight_ref[:, here : here + lanes]

    shape = (count, rows, groups * width)
    return kernel_call(
        kernel,
        out_shape=jax.ShapeDtypeStruct(shape, weight.dtype),
        grid_spec=pltpu.PrefetchScalarGridSpec(
            num_scalar_prefetch=1,
            grid=(1,),
            in_specs=[pl.BlockSpec((rows, weight.shape[1]), lambda i, at: (at[0], 0))],
            out_specs=pl.BlockSpec(shape, lambda i, at: (0, 0, 0)),
        ),
        name="select_rows",
    )(scalar(replica), weight)


def join_weight(pieces, bits, replica):
    count, rows, columns = pieces[0].shape
    copies = len(pieces)

    def kernel(at, *refs):
        for p in range(copies):
            q = pl.multiple_of((at[0] ^ p) * rows, rows)
            refs[-1][0, pl.ds(q, rows), :] = refs[p][0]

    return kernel_call(
        kernel,
        out_shape=jax.ShapeDtypeStruct((count, copies * rows, columns), pieces[0].dtype),
        grid_spec=pltpu.PrefetchScalarGridSpec(
            num_scalar_prefetch=1,
            grid=(count,),
            in_specs=[pl.BlockSpec((1, rows, columns), lambda i, at: (i, 0, 0))] * copies,
            out_specs=pl.BlockSpec((1, copies * rows, columns), lambda i, at: (i, 0, 0)),
        ),
        name="join_weight",
    )(scalar(replica), *pieces).reshape(count * copies * rows, columns)


def join_rows(pieces, heights, bits, replica):
    rows, columns = pieces[0].shape
    copies, order, block = len(pieces), replica_order(bits), min(512, columns)
    steps = columns // block

    def kernel(at, *refs):
        outs, start = refs[copies:], 0
        for out, height in zip(outs, heights):
            for side in range(2):

                @pl.when(pl.program_id(0) == side)
                def _():
                    for p, ref in zip(order, refs):
                        q = pl.multiple_of((at[0] ^ p) * height, height)
                        at_row = start + side * height
                        out[pl.ds(q, height), :] = ref[at_row : at_row + height, :].astype(F32)

            start += 2 * height

    return kernel_call(
        kernel,
        out_shape=tuple(jax.ShapeDtypeStruct((copies * h, 2 * columns), F32) for h in heights),
        grid_spec=pltpu.PrefetchScalarGridSpec(
            num_scalar_prefetch=1,
            grid=(2, steps),
            in_specs=[pl.BlockSpec((rows, block), lambda s, i, at: (0, i))] * copies,
            out_specs=[
                pl.BlockSpec((copies * h, block), lambda s, i, at: (0, s * steps + i))
                for h in heights
            ],
        ),
        compiler_params=pltpu.CompilerParams(vmem_limit_bytes=40 * 2**20),
        name="join_rows",
    )(scalar(replica), *pieces)


def join_grad(pieces, bits, replica, groups, cost=1):
    count, rows, columns = pieces[0].shape
    copies, width = len(pieces), columns // groups
    order = replica_order(bits)
    lanes = width if groups == 1 else 2 * HD
    halves = width // lanes
    if groups == 1:
        grid, batch = (count, 1), 1
        ins = pl.BlockSpec((1, rows, width), lambda i, h, at: (i, 0, 0))
        out = pl.BlockSpec((copies * rows, width), lambda i, h, at: (0, i))
    else:
        grid, batch = (groups, halves), count
        ins = pl.BlockSpec((count, rows, lanes), lambda g, h, at: (0, 0, h * groups + g))
        out = pl.BlockSpec((copies * rows, count * width), lambda g, h, at: (0, g))

    def kernel(at, *refs):
        for h in range(halves):

            @pl.when(pl.program_id(1) == h)
            def _():
                for p, ref in zip(order, refs):
                    q = pl.ds(pl.multiple_of((at[0] ^ p) * rows, rows), rows)
                    for i in range(batch):
                        to = i * width + h * lanes
                        refs[-1][q, to : to + lanes] = ref[i].astype(F32)

    return kernel_call(
        kernel,
        out_shape=jax.ShapeDtypeStruct((copies * rows, groups * count * width), F32),
        grid_spec=pltpu.PrefetchScalarGridSpec(
            num_scalar_prefetch=1, grid=grid, in_specs=[ins] * copies, out_specs=out
        ),
        cost=cost,
        name="join_grad",
    )(scalar(replica), *pieces)


def norm_tokens(gathered, shard, rows, width):
    count = gathered.shape[0]
    lanes = 2 * HD

    def kernel(shard_ref, x_ref, small_ref,
               out_ref, gain_ref, shift_ref, bias_ref, attn_ref, all_ref):
        @pl.when(pl.program_id(0) == 0)
        def _():
            for b in range(count):
                row = small_ref[b].astype(F32)[:1]
                at = pl.ds(b * width, width)
                gain_ref[:, at] = row[:, :width]
                shift_ref[:, at] = row[:, width : 2 * width]
                bias_ref[:, at] = row[:, 5 * width : 6 * width] + row[:, 6 * width : 7 * width]
                all_ref[:, b * 3 * width : (b + 1) * 3 * width] = row[:, 2 * width : 5 * width]
            for t in range(3):
                for h in range(width // lanes):
                    at = pl.multiple_of(t * D + shard_ref[0] * width + h * lanes, lanes)
                    to = (h * 3 + t) * lanes
                    attn_ref[:, to : to + lanes] = all_ref[:, pl.ds(at, lanes)]

        xhat, _ = normalize(x_ref[0].astype(F32))
        out_ref[...] = (xhat * gain_ref[...] + shift_ref[...]).astype(BF16)

    once = pl.BlockSpec((1, D), lambda j, shard: (0, 0))
    vector = jax.ShapeDtypeStruct((1, D), F32)
    tokens = jax.ShapeDtypeStruct((count * rows, D), BF16)
    return kernel_call(
        kernel,
        out_shape=(tokens, vector, vector, vector, jax.ShapeDtypeStruct((1, 3 * width), F32)),
        grid_spec=pltpu.PrefetchScalarGridSpec(
            num_scalar_prefetch=1,
            grid=(count,),
            in_specs=[
                pl.BlockSpec((1, rows, D), lambda j, shard: (j, 0, 0)),
                pl.BlockSpec((count, 16, D), lambda j, shard: (0, 2 * rows // 16, 0)),
            ],
            out_specs=[pl.BlockSpec((rows, D), lambda j, shard: (j, 0))]
            + [once] * 3
            + [pl.BlockSpec((1, 3 * width), lambda j, shard: (0, 0))],
            scratch_shapes=[pltpu.VMEM((1, 3 * D), F32)],
        ),
        name="norm_tokens",
    )(scalar(shard), gathered, gathered)


def weight_grad(tokens, grads, replica, first, count, copies, bits):
    size, columns = grads.shape
    width = tokens.shape[1] // lax.axis_size("shard")
    rows = width // copies
    order = replica_order(bits)

    def kernel(at, left, right, keep, send, whole):
        whole[...] = dot(left[...], right[...], (0, 0)).astype(BF16)
        for i, p in enumerate(order):
            piece = whole[pl.ds(pl.multiple_of((at[0] ^ p) * rows, rows), rows), :]
            (keep, send)[i // (copies // 2)][i % (copies // 2)] = piece

    out = pl.BlockSpec((copies // 2, rows, columns), lambda s, at: (0, s, 0))
    return kernel_call(
        kernel,
        out_shape=(jax.ShapeDtypeStruct((copies // 2, count * rows, columns), BF16),) * 2,
        grid_spec=pltpu.PrefetchScalarGridSpec(
            num_scalar_prefetch=1,
            grid=(count,),
            in_specs=[
                pl.BlockSpec((size, width), lambda s, at: (0, first + s)),
                pl.BlockSpec((size, columns), lambda s, at: (0, 0)),
            ],
            out_specs=[out] * 2,
            scratch_shapes=[pltpu.VMEM((width, columns), BF16)],
        ),
        compiler_params=pltpu.CompilerParams(vmem_limit_bytes=40 * 2**20),
        name="weight_grad",
    )(scalar(replica), tokens, grads)


def cotangent_spec(gathered, columns=D, buffered=1):
    shape = (gathered.shape[0], gathered.shape[1] // 2 // 16 * 16, columns)
    return pl.BlockSpec(shape, lambda i, *at: (0, 1, 0), pipeline_mode=pl.Buffered(buffered))


def flat(ref):
    shape = ref.shape
    return ref[...].reshape(shape[0] * shape[1], shape[2])


def row_grad(left, gathered, replica, copies, orders):
    size, rows = left.shape
    part, half = rows // copies, copies // 2
    places = [replica_order(bits) for bits in orders]
    steps = copies if part % 128 == 0 else 1
    height = part if len(orders) == 2 else 2 * part

    def kernel(at, left, right, *refs):
        outs, whole = refs[:-1], refs[-1]

        def put(p, piece):
            for h in range(2):
                order, to = (places * 2)[h], (2 * h if len(orders) == 2 else 0)
                i, top = order.index(p), h * part if len(orders) == 1 else 0
                columns = piece[:, h * D // 2 : (h + 1) * D // 2]
                outs[to + i // half][i % half, top : top + part] = columns

        product = dot(left[...], flat(right), (0, 0)).astype(BF16)
        if steps == 1:
            whole[...] = product
            for p in range(copies):
                put(p, whole[pl.ds(pl.multiple_of((at[0] ^ p) * part, part), part), :])
            return
        for p in range(copies):
            pl.when(pl.program_id(0) == p)(functools.partial(put, p, product))

    shape = (half, height, D // 2)
    return kernel_call(
        kernel,
        out_shape=(jax.ShapeDtypeStruct(shape, BF16),) * (2 * len(orders)),
        grid_spec=pltpu.PrefetchScalarGridSpec(
            num_scalar_prefetch=1,
            grid=(steps,),
            in_specs=[
                pl.BlockSpec((size, rows // steps), lambda i, at: (0, (at[0] ^ i) % steps)),
                cotangent_spec(gathered),
            ],
            out_specs=[pl.BlockSpec(shape, lambda i, at: (0, 0, 0))] * (2 * len(orders)),
            scratch_shapes=[pltpu.VMEM((rows if steps == 1 else 16, D), BF16)],
        ),
        compiler_params=pltpu.CompilerParams(vmem_limit_bytes=48 * 2**20),
        name="row_grad",
    )(scalar(replica), left, gathered)


def feed_forward(normed, gathered, up, down, bias):
    size, ff = normed.shape[0], up.shape[1]
    block = 256
    step, parts = size // (size // 512), size // 512
    shards = gathered.shape[0] // parts

    def kernel(x, g, u, d, b, hidden, grad, total):
        total[...] = jnp.zeros_like(total)
        for i in range(parts):
            at = pl.ds(i * step, step)
            value, slope = gelu_and_slope(dot(x[at, :], u[...]) + b[...])
            hidden[at, :] = value.astype(BF16)
            up_to = g[i * shards : (i + 1) * shards].reshape(step, D)
            low = (dot(up_to, d[...], (1, 1)) * slope).astype(BF16)
            grad[at, :] = low
            total[...] += jnp.sum(low.astype(F32), axis=0, keepdims=True)

    whole = pl.BlockSpec((size, D), lambda f: (0, 0), pipeline_mode=pl.Buffered(1))
    column = pl.BlockSpec((size, block), lambda f: (0, f))
    vector = pl.BlockSpec((1, block), lambda f: (0, f))
    shape = jax.ShapeDtypeStruct((size, ff), BF16)
    return kernel_call(
        kernel,
        out_shape=(shape, shape, jax.ShapeDtypeStruct((1, ff), F32)),
        grid=(ff // block,),
        in_specs=[
            whole,
            cotangent_spec(gathered),
            pl.BlockSpec((D, block), lambda f: (0, f)),
            pl.BlockSpec((block, D), lambda f: (f, 0)),
            vector,
        ],
        out_specs=[column, column, vector],
        compiler_params=pltpu.CompilerParams(vmem_limit_bytes=50 * 2**20),
        name="feed_forward",
    )(normed, gathered, up, down, bias)


def project(normed, gathered, pieces, bias, dense, replica):
    count, rows, columns = pieces[0].shape
    copies, size, width = len(pieces), normed.shape[0], dense.shape[0]
    step = size // count

    def kernel(at, x, g, d, b, *refs):
        weight, out, grad = refs[copies:]

        @pl.when(pl.program_id(0) == 0)
        def _():
            for i in range(count):
                for p in range(copies):
                    q = pl.multiple_of((i * copies + (at[0] ^ p)) * rows, rows)
                    weight[pl.ds(q, rows), :] = refs[p][i]

        out[...] = dot(x[...], weight[...]) + b[...]
        grad[...] = dot(flat(g), d[...], (1, 1)).astype(BF16)

    def once(shape):
        zeros = (0,) * len(shape)
        return pl.BlockSpec(shape, lambda i, at: zeros, pipeline_mode=pl.Buffered(1))

    pair = 2
    tokens = gathered.shape[1] // 2 // 16 * 16
    return kernel_call(
        kernel,
        out_shape=(
            jax.ShapeDtypeStruct((D, columns), BF16),
            jax.ShapeDtypeStruct((size, columns), F32),
            jax.ShapeDtypeStruct((size, width), BF16),
        ),
        grid_spec=pltpu.PrefetchScalarGridSpec(
            num_scalar_prefetch=1,
            grid=(count // pair,),
            in_specs=[
                pl.BlockSpec((pair * step, D), lambda i, at: (i, 0)),
                pl.BlockSpec((pair, tokens, D), lambda i, at: (i, 1, 0)),
                once((width, D)),
                once((1, columns)),
            ]
            + [once((count, rows, columns))] * copies,
            out_specs=[
                once((D, columns)),
                pl.BlockSpec((pair * step, columns), lambda i, at: (i, 0)),
                pl.BlockSpec((pair * step, width), lambda i, at: (i, 0)),
            ],
        ),
        compiler_params=pltpu.CompilerParams(vmem_limit_bytes=40 * 2**20),
        name="project",
    )(scalar(replica), normed, gathered, dense, bias, *pieces)


def token_products(grad_projected, attn, grad_pre, up, hidden, down, mixed, dense):
    size = grad_pre.shape[0]
    step = min(256, size)

    def kernel(ga, wa, gu, wu, h, wd, m, wo, out):
        out[:, :D] = (
            dot(ga[...], wa[...], (1, 1)) + dot(gu[...], wu[...], (1, 1))
        ).astype(BF16)
        out[:, D:] = (dot(h[...], wd[...]) + dot(m[...], wo[...])).astype(BF16)

    def part(array):
        return pl.BlockSpec((step, array.shape[1]), lambda i: (i, 0))

    def whole(array):
        return pl.BlockSpec(array.shape, lambda i: (0, 0), pipeline_mode=pl.Buffered(1))

    args = (grad_projected, attn, grad_pre, up, hidden, down, mixed, dense)
    return kernel_call(
        kernel,
        out_shape=jax.ShapeDtypeStruct((size, 2 * D), BF16),
        grid=(size // step,),
        in_specs=[(part, whole)[i % 2](array) for i, array in enumerate(args)],
        out_specs=pl.BlockSpec((step, 2 * D), lambda i: (i, 0)),
        compiler_params=pltpu.CompilerParams(vmem_limit_bytes=48 * 2**20),
        cost=HUGE,
        name="token_products",
    )(*args)


def attention_kernel(
    q_ref, k_ref, v_ref, g_ref, cos_ref, lo_ref, hi_ref,
    mix_ref, grad_ref, sum_ref,
    q_sc, k_sc, v_sc, dk_sc, dv_sc,
    *, tokens, step,
):
    scale = HD**-0.5
    lanes = 2 * HD

    def turn(x, at, sign):
        cos, lo, hi = cos_ref[at, :], lo_ref[at, :], hi_ref[at, :]
        up = pltpu.roll(x, lanes - ROT // 2, 1)
        down = pltpu.roll(x, ROT // 2, 1)
        return x * cos + sign * (up * lo + down * hi)

    blocks = [pl.ds(i * step, step) for i in range(tokens // step)]
    for at in blocks:
        q_sc[at, :] = turn(q_ref[at, :], at, 1.0).astype(BF16)
        k_sc[at, :] = turn(k_ref[at, :], at, 1.0).astype(BF16)
        v_sc[at, :] = v_ref[at, :].astype(BF16)
    dk_sc[...] = jnp.zeros_like(dk_sc)
    dv_sc[...] = jnp.zeros_like(dv_sc)
    lane = lax.broadcasted_iota(jnp.int32, (1, lanes), 1)
    heads = [lane < HD, lane >= HD]
    for i, rows in enumerate(blocks):
        width = (i + 1) * step
        q, g = q_sc[rows, :], g_ref[rows, :]
        k, v = k_sc[:width, :], v_sc[:width, :]
        seen = lax.broadcasted_iota(jnp.int32, (step, width), 1) <= i * step + (
            lax.broadcasted_iota(jnp.int32, (step, width), 0)
        )
        mixed = jnp.zeros((step, lanes), F32)
        dq = jnp.zeros((step, lanes), F32)
        for mine in heads:
            zero = jnp.zeros((), BF16)
            qh, gh = jnp.where(mine, q, zero), jnp.where(mine, g, zero)
            scores = dot(qh, k, (1, 1)) * scale
            scores = jnp.where(seen, scores, MASK_VALUE)
            top = jnp.max(scores, axis=1, keepdims=True)
            raised = jnp.exp(scores - top)
            probs = raised / jnp.sum(raised, axis=1, keepdims=True)
            weights = probs.astype(BF16)
            mixed = jnp.where(mine, dot(weights, v), mixed)
            grad_probs = dot(gh, v, (1, 1))
            delta = jnp.sum(probs * grad_probs, axis=1, keepdims=True)
            grad_scores = (probs * (grad_probs - delta)).astype(BF16)
            dq = jnp.where(mine, dot(grad_scores, k), dq)
            dk_sc[:width, :] += dot(grad_scores, qh, (0, 0))
            dv_sc[:width, :] += dot(weights, gh, (0, 0))
        mix_ref[rows, :] = mixed.astype(BF16)
        grad_ref[rows, :lanes] = turn(dq * scale, rows, -1.0).astype(BF16)
    for at in blocks:
        grad_ref[at, lanes : 2 * lanes] = turn(dk_sc[at, :] * scale, at, -1.0).astype(BF16)
        grad_ref[at, 2 * lanes :] = dv_sc[at, :].astype(BF16)
    sum_ref[...] = jnp.zeros_like(sum_ref)
    for at in blocks:
        sum_ref[...] += jnp.sum(grad_ref[at, :].astype(F32), axis=0, keepdims=True)


def rope_tables(tokens):
    half = ROT // 2
    frequencies = np.float32(ROPE_BASE) ** (-2.0 * np.arange(half, dtype=np.float32) / ROT)
    angles = np.arange(tokens, dtype=np.float32)[:, None] * frequencies.astype(np.float32)[None]
    cosine, sine = np.cos(angles.astype(np.float64)), np.sin(angles.astype(np.float64))
    none, rest = np.zeros_like(sine), np.zeros((tokens, HD - ROT))
    tables = ([cosine, cosine, rest + 1.0], [-sine, none, rest], [none, sine, rest])
    return [np.concatenate(t * 2, axis=1).astype(np.float32) for t in tables]


def attention(projected, grad_mixed):
    tokens, width = grad_mixed.shape
    lanes = 2 * HD

    def column(stride, offset):
        return pl.BlockSpec((tokens, lanes), lambda h: (0, stride * h + offset))

    whole = pl.BlockSpec((tokens, lanes), lambda h: (0, 0))
    return kernel_call(
        functools.partial(attention_kernel, tokens=tokens, step=min(256, tokens)),
        out_shape=(
            jax.ShapeDtypeStruct((tokens, width), BF16),
            jax.ShapeDtypeStruct((tokens, 3 * width), BF16),
            jax.ShapeDtypeStruct((1, 3 * width), F32),
        ),
        grid=(width // lanes,),
        in_specs=[column(3, 0), column(3, 1), column(3, 2), column(1, 0), whole, whole, whole],
        out_specs=[
            column(1, 0),
            pl.BlockSpec((tokens, 3 * lanes), lambda h: (0, h)),
            pl.BlockSpec((1, 3 * lanes), lambda h: (0, h)),
        ],
        scratch_shapes=[pltpu.VMEM((tokens, lanes), BF16)] * 3
        + [pltpu.VMEM((tokens, lanes), F32)] * 2,
        compiler_params=pltpu.CompilerParams(vmem_limit_bytes=48 * 2**20),
        name="attention",
    )(projected, projected, projected, grad_mixed, *map(jnp.asarray, rope_tables(tokens)))


def group_sums(sums, groups):
    lanes, columns = 2 * HD, sums.shape[1]
    parts = columns // groups // lanes

    def kernel(ref, out):
        for h in range(parts):
            for g in range(groups):
                to, at = (g * parts + h) * lanes, (h * groups + g) * lanes
                out[:, to : to + lanes] = ref[:, at : at + lanes]

    return kernel_call(
        kernel, out_shape=jax.ShapeDtypeStruct(sums.shape, F32), cost=MEDIUM, name="group_sums"
    )(sums)


def finish(own, upstream, part, gain, out_bias, sum_attn, shard, count):
    width = D // count

    def kernel(at, x_ref, g_ref, part_ref, gain_ref, bias_ref, attn_ref, out, grad, sums):
        inputs, cotangent = x_ref[...].astype(F32), g_ref[...].astype(F32)
        out[...] = (inputs + part_ref[:, D:].astype(F32) + bias_ref[...]).astype(BF16)
        rows = part_ref[:, :D].astype(F32)
        xhat, inverse = normalize(inputs)
        scaled = rows * gain_ref[...]
        mean = jnp.mean(scaled, axis=-1, keepdims=True)
        along = jnp.mean(scaled * xhat, axis=-1, keepdims=True)
        grad[...] = (cotangent + inverse * (scaled - mean - xhat * along)).astype(BF16)
        for i, term in enumerate((rows * xhat, rows, cotangent)):
            total = jnp.sum(term, axis=0, keepdims=True)
            for j in range(count):
                sums[j : j + 1, i * width : (i + 1) * width] = total[:, j * width : (j + 1) * width]
        for slot in range(3):
            block = 3 * lax.broadcasted_iota(jnp.int32, (count, width), 0) + slot
            here = jnp.zeros((count, width), F32)
            for t in range(3):
                term = attn_ref[:, t * width : (t + 1) * width]
                here = jnp.where(block == t * count + at[0], term, here)
            sums[:, (3 + slot) * width : (4 + slot) * width] = here

    tokens = jax.ShapeDtypeStruct(own.shape, BF16)
    vmem = pl.BlockSpec(memory_space=pltpu.VMEM)
    return kernel_call(
        kernel,
        out_shape=(tokens, tokens, jax.ShapeDtypeStruct((count, 6 * width), F32)),
        in_specs=[pl.BlockSpec(memory_space=pltpu.SMEM)] + [vmem] * 6,
        out_specs=[vmem] * 3,
        compiler_params=pltpu.CompilerParams(vmem_limit_bytes=40 * 2**20),
        name="finish",
    )(scalar(shard), own, upstream, part, gain, out_bias, sum_attn)


def normalize(values):
    center = values - jnp.mean(values, axis=-1, keepdims=True)
    spread = jnp.mean(center * center, axis=-1, keepdims=True)
    inverse = lax.rsqrt(spread + EPSILON)
    return center * inverse, inverse


def gelu_and_slope(u):
    inner = GELU_C * (u + 0.044715 * u * u * u)
    t = jnp.tanh(inner)
    slope = 0.5 * (1.0 + t) + 0.5 * u * (1.0 - t * t) * GELU_C * (1.0 + 3 * 0.044715 * u * u)
    return 0.5 * u * (1.0 + t), slope


def shards(
    block_in,
    norm_gain,
    norm_bias,
    attn_weight,
    attn_bias,
    dense_weight,
    dense_bias,
    up_weight,
    up_bias,
    down_weight,
    down_bias,
    cotangent,
):
    own, upstream = block_in[0], cotangent[0]
    tok_rows = own.shape[0]
    count, copies = lax.axis_size("shard"), lax.axis_size("replica")
    shard, replica = lax.axis_index("shard"), lax.axis_index("replica")
    width = attn_weight.shape[0]
    ff = down_weight.shape[0]
    part_rows = width // copies
    bits = list(range(copies.bit_length() - 1))
    back = bits[::-1]

    small = jnp.concatenate(
        [norm_gain, norm_bias, attn_bias, dense_bias, down_bias, jnp.zeros((D - 7 * width,), BF16)]
    )
    packed = jnp.concatenate([own, upstream, jnp.broadcast_to(small[None], (16, D))], axis=0)
    up_part = exchange(select_rows(up_weight, replica, count, copies, 1))
    gathered = lax.all_gather(after(packed, up_part), "shard", axis=0)
    attn_part = exchange(after(select_rows(attn_weight, replica, count, copies, 3), up_part))
    up_mine = join_weight(spread_replicas(up_part), bits, replica)
    attn_pieces = spread_replicas(after(attn_part, up_mine))
    gathered = after(gathered, up_mine, *attn_pieces)
    normed, gain, shift, out_bias, attn_bias_mine = norm_tokens(gathered, shard, tok_rows, width)

    hidden, grad_pre, sum_up = feed_forward(
        normed, gathered, up_mine, down_weight, up_bias.astype(F32)[None]
    )
    half, orders = count // 2, (bits, back)

    def split(kernel_outs):
        return list(kernel_outs[:2]), list(kernel_outs[2:])

    def two_halves(grads):
        first = weight_grad(normed, grads, replica, 0, half, copies, bits)
        second = weight_grad(normed, after(grads, *first), replica, half, half, copies, back)
        return [first, second]

    def cross_both(pairs, *hold):
        return [cross(pair, order[0], *hold) for pair, order in zip(pairs, orders)]

    up_pairs = two_halves(grad_pre)
    down_pairs = split(
        row_grad(after(hidden, *up_pairs[1]), gathered, replica, copies, orders)
    )

    attn_mine, projected, grad_mixed = project(
        after(normed, *down_pairs[1]), gathered, attn_pieces, attn_bias_mine, dense_weight, replica
    )
    up_pairs = [add([terms]) for terms in cross_both(up_pairs, projected)]
    projected = after(projected, *up_pairs[0], *up_pairs[1])
    mixed, grad_projected, sum_attn = attention(projected, grad_mixed)
    dense_pair = row_grad(mixed, gathered, replica, copies, (back,))
    (grad_up,) = add(last_pairs(up_pairs, orders, *dense_pair))
    grad_up = grad_up.reshape(count, part_rows, ff)
    attn_pairs = two_halves(after(grad_projected, grad_up))
    grad_up = exchange(grad_up)

    rest = after(grad_projected, *attn_pairs[1])
    part = token_products(
        rest, attn_mine, grad_pre, up_mine, hidden, down_weight, mixed, dense_weight
    )
    own_part = lax.psum_scatter(part, "shard", scatter_dimension=0, tiled=True)
    grad_up = after(grad_up, part)

    first, second = cross_both(down_pairs, part, grad_up)
    rows_pairs = [add([first], HUGE), add([second, cross(dense_pair, back[0], part)])]
    attn_pairs = [add([terms]) for terms in cross_both(attn_pairs, *rows_pairs[1])]
    (grad_rows,) = add(last_pairs(rows_pairs, orders, *attn_pairs[1]))
    grad_rows = grad_rows[0]
    (grad_attn,) = add(last_pairs(attn_pairs, orders, grad_rows), MEDIUM)
    grad_attn = grad_attn.reshape(count, part_rows, 3 * width)
    sum_attn = group_sums(after(sum_attn, grad_attn), 3)
    grad_attn = after(exchange(grad_attn), sum_attn)
    up_pieces = gather_replicas(grad_up, bits)
    row_pieces = gather_replicas(grad_rows, back)
    down_whole, dense_whole = join_rows(row_pieces, (ff // copies, part_rows), back, replica)

    block_out, grad_in, sums = finish(
        own, upstream, after(own_part, grad_attn), gain, out_bias, sum_attn, shard, count
    )

    sums = jnp.sum(exchange(sums), axis=0)
    sums = sum(spread_replicas(jnp.concatenate([sums, sum_up[0]])))
    grad_out_bias = sums[2 * width : 3 * width]
    attn_pieces = gather_replicas(grad_attn, bits, grad_in)
    up_whole = join_grad([after(a, down_whole) for a in up_pieces], bits, replica, 1)
    attn_whole = join_grad([after(a, up_whole) for a in attn_pieces], bits, replica, 3)
    return (
        block_out[None],
        grad_in[None],
        sums[:width],
        sums[width : 2 * width],
        attn_whole,
        sums[3 * width : 6 * width],
        dense_whole,
        grad_out_bias,
        up_whole,
        sums[6 * width :],
        down_whole,
        grad_out_bias,
    )


def solution(mesh):
    vector, matrix = P("shard"), P("shard", None)
    rows = P("replica", "shard", None)
    return jax.shard_map(
        shards,
        mesh=mesh,
        in_specs=(rows, vector, vector, matrix, vector, matrix, vector, matrix, vector, matrix, vector, rows),
        out_specs=(rows, rows, vector, vector, matrix, vector, matrix, vector, matrix, vector, matrix, vector),
        check_vma=False,
    )
```
